32 devices in a mesh: seq: 8 (over z, y), head: 4 (over x, core).
Axes of the slice: x: 2, y: 2, z: 4, core: 2. Of those that a mesh axis runs over, the one named last changes fastest.
Arguments:
- q_latent: bfloat16 [1024, 32, 576], P('seq', 'head'), may hold values from -6 to 6
- kv_latent: bfloat16 [1024, 576], P('seq'), may hold values from -6 to 6
- normalizer: float32 [1024, 32], P('seq', 'head'), may hold values from 3 to 8
- q_index: bfloat16 [1024, 16, 128], P('seq', 'head'), may hold values from -0.5 to 0.5
- k_index: bfloat16 [1024, 128], P('seq'), may hold values from -6 to 6
- index_weight: float32 [1024, 16], P('seq', 'head'), may hold values from -6 to 6
- span_pos: int32 [16], replicated, may hold values from 0 to 15, each once
Outputs:
- grad_query: float32 [1024, 16, 128], P('seq', 'head')
- grad_weight: float32 [1024, 16], P('seq', 'head')
- grad_key: float32 [1024, 128], P('seq')
The draws below stay inside these ranges and needn't reach their ends.
Inputs may be any that keep to these rules, and one draw needn't show every extreme that they name: `span_pos`: each span position appears exactly once.
All inputs are finite; a program needn't handle non-finite values.
Results may differ from the reference program's by a relative error of at most 0.0085.
Values may be sent and summed in bfloat16 or wider, within the bound.
A program may use at most 64 MiB of HBM per device.

```python
import jax
import jax.numpy as jnp
from jax import lax

LATENT = 576
IDIM = 128
HEAD_DEV = 8
Q_DEV = 128
HEADS = 32
IHEADS = 16
SEQ = 1024
SPAN = 64
SPANS = 16
N_SEQ = 8


def draw_index_weight(key, part):
    key_one = jax.random.fold_in(jax.random.fold_in(key, 17), 0)
    values = jnp.clip(jax.random.normal(key_one, (SEQ, IHEADS), jnp.float32), -6.0, 6.0)
    return values.astype(jnp.float32)


def level_of(own_key, dims, pieces, low, largest):
    loudness = 1.0
    for dim, shards_of in pieces:
        draws = jax.random.uniform(jax.random.fold_in(jax.random.fold_in(own_key, 6), dim), (shards_of,), jnp.float32, low / len(pieces), largest / len(pieces))
        loudness = loudness * jnp.repeat(jnp.exp(draws), dims[dim] // shards_of).reshape((-1,) + (1,) * (len(dims) - 1 - dim))
    return loudness


def normal_values(own_key, dims, spread, most, shards=(), held_as=jnp.bfloat16):
    gain = level_of(own_key, dims, shards, -0.22, 0.18) if shards else 1.0
    entries = jax.random.normal(own_key, dims, jnp.float32) * spread * gain
    return jnp.minimum(jnp.maximum(entries, -most), most).astype(held_as)


def setup_inputs(seed: int = 0) -> dict:
    seeds = jax.random.split(jax.random.key(seed), 8)
    return {
        "q_latent": normal_values(seeds[0], (SEQ, HEADS, LATENT), 1.0, 6.0, ((0, 8), (1, 4))),
        "kv_latent": normal_values(seeds[1], (SEQ, LATENT), 1.0, 6.0, ((0, 8),)),
        "normalizer": jnp.clip(3.0 + 5.0 * jax.random.uniform(seeds[2], (SEQ, HEADS), jnp.float32) ** level_of(seeds[2], (SEQ, HEADS), ((0, 8), (1, 4)), -0.2, 0.2), 3.0, 8.0),
        "q_index": normal_values(seeds[3], (SEQ, IHEADS, IDIM), IDIM ** -0.5, 0.5, ((0, 8), (1, 4))),
        "k_index": normal_values(seeds[4], (SEQ, IDIM), 1.0, 6.0, ((0, 8),)),
        "index_weight": draw_index_weight(jax.random.fold_in(seeds[7], 71), 0),
        "span_pos": jax.random.permutation(seeds[6], SPANS).astype(jnp.int32),
    }


softmax_scale = 192.0 ** -0.5


def positions(span_pos):
    offsets = jnp.arange(SPAN, dtype=jnp.int32)
    return (span_pos[:, None] * SPAN + offsets[None, :]).reshape(-1).astype(jnp.int32)


def reference(q_latent, kv_latent, normalizer, q_index, k_index, index_weight, span_pos):
    token_pos = positions(span_pos)
    latent_keys = kv_latent.astype(jnp.float32)
    index_keys = k_index.astype(jnp.float32)
    groups = HEADS // HEAD_DEV

    def one_block(key_grad, block_index):
        first_row = (block_index * Q_DEV).astype(jnp.int32)
        queries = lax.dynamic_slice_in_dim(q_latent, first_row, Q_DEV, 0).astype(jnp.float32)
        stored = lax.dynamic_slice_in_dim(normalizer, first_row, Q_DEV, 0)
        index_queries = lax.dynamic_slice_in_dim(q_index, first_row, Q_DEV, 0).astype(jnp.float32)
        weights = lax.dynamic_slice_in_dim(index_weight, first_row, Q_DEV, 0)
        query_pos = lax.dynamic_slice_in_dim(token_pos, first_row, Q_DEV, 0)
        visible = token_pos[None, :] <= query_pos[:, None]
        grouped_q = queries.reshape(Q_DEV, groups, HEAD_DEV, LATENT).transpose(1, 0, 2, 3)
        grouped_l = stored.reshape(Q_DEV, groups, HEAD_DEV).transpose(1, 2, 0)

        def one_group(total, inputs):
            group_q, group_l = inputs
            scores = jnp.einsum('qhl,kl->hqk', group_q, latent_keys, precision=lax.Precision.HIGHEST) * softmax_scale
            attention = jnp.where(visible[None], jnp.exp(scores - group_l[:, :, None]), 0.0)
            partial_sum = jnp.sum(attention, axis=0)
            rounded = lax.optimization_barrier(partial_sum.astype(jnp.bfloat16)).astype(jnp.float32)
            return total + rounded, None

        target_raw, _ = lax.scan(one_group, jnp.zeros((Q_DEV, SEQ), jnp.float32), (grouped_q, grouped_l))
        target = target_raw / jnp.sum(target_raw, axis=1)[:, None]
        index_score = jnp.einsum('qhd,kd->hqk', index_queries, index_keys, precision=lax.Precision.HIGHEST)
        rectified = jnp.maximum(index_score, 0.0)
        logit = jnp.sum(weights.T[:, :, None] * rectified, axis=0)
        row_peak = jnp.max(jnp.where(visible, logit, -jnp.inf), axis=1)
        expo = jnp.where(visible, jnp.exp(logit - row_peak[:, None]), 0.0)
        prob = expo / jnp.sum(expo, axis=1)[:, None]
        delta = lax.optimization_barrier((prob - target).astype(jnp.bfloat16)).astype(jnp.float32)
        grad_weight = jnp.sum(delta[None] * rectified, axis=2).T
        delta_index = jnp.where(index_score > 0, delta[None] * weights.T[:, :, None], 0.0)
        delta_index = lax.optimization_barrier(delta_index.astype(jnp.bfloat16)).astype(jnp.float32)
        grad_query = jnp.einsum('hqk,kd->qhd', delta_index, index_keys, precision=lax.Precision.HIGHEST)
        key_grad = key_grad + jnp.einsum('hqk,qhd->kd', delta_index, index_queries, precision=lax.Precision.HIGHEST)
        return key_grad, (grad_query, grad_weight)

    key_grad, (grad_query, grad_weight) = lax.scan(one_block, jnp.zeros((SEQ, IDIM), jnp.float32), jnp.arange(N_SEQ, dtype=jnp.int32))
    return grad_query.reshape(SEQ, IHEADS, IDIM), grad_weight.reshape(SEQ, IHEADS), key_grad
```

```python
import functools

import jax
import jax.numpy as jnp
from jax import lax
from jax.experimental import pallas as pl
from jax.experimental.pallas import tpu as pltpu
from jax.sharding import PartitionSpec as P

MESH = pl.DeviceIdType.MESH
F32 = jnp.float32
BF16 = jnp.bfloat16
softmax_scale = 192.0 ** (-0.5)


def kernel(
    n, m, heads, iheads, span,
    q_ref, kv_ref, norm_ref, qi_ref, ki_ref, w_ref, span_ref,
    gq_ref, gw_ref, gk_ref,
    kvbuf, kibuf, normb, wb, attn, wscore, iscore, lbuf, tbuf, l1, t1, l2, t2, lx, tx,
    lall, tall, dbuf, dall, gwacc, gkbuf, gkrecv, hbuf,
    ring_send, ring_recv, core_send, core_recv, s1_send, s1_recv, s2_send, s2_recv,
    d_send, d_recv, gk_send, gk_recv, h_send, h_recv,
):
    s = lax.axis_index("seq")
    h = lax.axis_index("head")
    half = kv_ref.shape[1]
    rows = 2 * half
    c = h % 2
    other = 1 - c
    partner = h + 1 - 2 * c
    near = n // 2

    def seq_at(pos):
        upper = pos // near
        return upper * (2 * (n - 1 - pos) + 1) + (1 - upper) * 2 * pos

    column = s % 2
    place = column * (n - 1 - s // 2) + (1 - column) * (s // 2)

    def seq_off(off):
        return seq_at((place + off + n) % n)

    barrier = pltpu.get_barrier_semaphore()
    for d in range(1, n):
        pl.semaphore_signal(barrier, inc=1, device_id=((s + d) % n, h), device_id_type=MESH)
    for d in range(1, m):
        pl.semaphore_signal(barrier, inc=1, device_id=(s, (h + d) % m), device_id_type=MESH)
    pl.semaphore_wait(barrier, n - 1 + m - 1)

    forward = n // 2
    backward = n - 1 - forward
    offsets = {0: 0}
    for k in range(1, forward + 1):
        offsets[k] = -k
    for k in range(1, backward + 1):
        offsets[forward + k] = k
    order = [0]
    for k in range(1, forward + 1):
        order.append(k)
        if k <= backward:
            order.append(forward + k)

    pending = []

    def remote(src, dst, send, recv, device):
        copy = pltpu.make_async_remote_copy(
            src_ref=src, dst_ref=dst, send_sem=send, recv_sem=recv,
            device_id=device, device_id_type=MESH,
        )
        copy.start()
        pending.append(copy)
        return copy

    def ring_copy(source, target, peer):
        if source == 0:
            kv_src, ki_src = kv_ref.at[c], ki_ref.at[c]
        else:
            kv_src, ki_src = kvbuf.at[source, c], kibuf.at[source, c]
        return (
            remote(kv_src, kvbuf.at[target, c], ring_send.at[target, 0],
                   ring_recv.at[target, 0], (peer, h)),
            remote(ki_src, kibuf.at[target, c], ring_send.at[target, 1],
                   ring_recv.at[target, 1], (peer, h)),
        )

    def core_copy(slot):
        return (
            remote(kvbuf.at[slot, c], kvbuf.at[slot, c], core_send.at[slot, 0],
                   core_recv.at[slot, 0], (s, partner)),
            remote(kibuf.at[slot, c], kibuf.at[slot, c], core_send.at[slot, 1],
                   core_recv.at[slot, 1], (s, partner)),
        )

    following, preceding = seq_off(1), seq_off(-1)
    ring = {1: ring_copy(0, 1, following)}
    if backward:
        ring[forward + 1] = ring_copy(0, forward + 1, preceding)
    kibuf[0] = ki_ref[...]

    for g in range(heads):
        normb[pl.ds(g, rows, stride=heads), :] = jnp.broadcast_to(norm_ref[:, g:g + 1], (rows, rows))
    for g in range(iheads):
        wb[pl.ds(g, rows, stride=iheads), :] = jnp.broadcast_to(w_ref[:, g:g + 1], (rows, rows))

    per_block = rows // span

    def positions(block, index):
        found = jnp.zeros(index.shape, jnp.int32)
        for t in range(per_block):
            base = span_ref[block * per_block + t]
            found = jnp.where(index // span == t, base * span + index % span, found)
        return found

    query_pos = positions(s, lax.broadcasted_iota(jnp.int32, (rows, rows), 0))
    half_pos = positions(s, lax.broadcasted_iota(jnp.int32, (half, rows), 0) + c * half)

    def key_pos(slot, count):
        return positions(seq_off(offsets[slot]), lax.broadcasted_iota(jnp.int32, (count, rows), 1))

    contract_last = (((1,), (1,)), ((), ()))

    def compute(slot):
        kv = (kv_ref[...] if slot == 0 else kvbuf[slot]).reshape(rows, kv_ref.shape[2])
        ki = kibuf[slot].reshape(rows, ki_ref.shape[2])
        scores = lax.dot_general(q_ref[...], kv, contract_last, preferred_element_type=F32)
        attn[...] = jnp.exp(scores * softmax_scale - normb[...])
        rectified = jnp.maximum(
            lax.dot_general(qi_ref[...], ki, contract_last, preferred_element_type=F32), 0.0
        )
        iscore[slot] = rectified
        wscore[...] = wb[...] * rectified
        total = attn[pl.ds(0, rows, stride=heads), :]
        for g in range(1, heads):
            total = total + attn[pl.ds(g, rows, stride=heads), :]
        logit = wscore[pl.ds(0, rows, stride=iheads), :]
        for g in range(1, iheads):
            logit = logit + wscore[pl.ds(g, rows, stride=iheads), :]
        total = jnp.where(key_pos(slot, rows) <= query_pos, total, 0.0).astype(BF16)
        lbuf[slot] = logit.reshape(2, half, rows)
        tbuf[slot] = total.reshape(2, half, rows)
        return (
            remote(lbuf.at[slot, other], l1.at[slot], s1_send.at[slot, 0],
                   s1_recv.at[slot, 0], (s, partner)),
            remote(tbuf.at[slot, other], t1.at[slot], s1_send.at[slot, 1],
                   s1_recv.at[slot, 1], (s, partner)),
        )

    def pair_sum(slot, copies):
        for copy in copies:
            copy.wait_recv()
        l2[slot] = lbuf[slot, c] + l1[slot]
        t2[slot] = (tbuf[slot, c].astype(F32) + t1[slot].astype(F32)).astype(BF16)
        out = []
        for r in range(1, m // 2):
            peer = (h + 2 * r) % m
            out.append(remote(l2.at[slot], lx.at[slot, r - 1], s2_send.at[slot, r - 1, 0],
                              s2_recv.at[slot, r - 1, 0], (s, peer)))
            out.append(remote(t2.at[slot], tx.at[slot, r - 1], s2_send.at[slot, r - 1, 1],
                              s2_recv.at[slot, r - 1, 1], (s, peer)))
        return out

    first = {0: compute(0)}
    second = {}
    last = 0
    for k in range(1, forward + 1):
        arrived = [k] + ([forward + k] if k <= backward else [])
        core = {}
        for slot in arrived:
            for copy in ring[slot]:
                copy.wait_recv()
            if slot <= forward and k < forward:
                ring[slot + 1] = ring_copy(slot, slot + 1, following)
            if slot > forward and k < backward:
                ring[slot + 1] = ring_copy(slot, slot + 1, preceding)
            core[slot] = core_copy(slot)
        for slot in arrived:
            for copy in core[slot]:
                copy.wait_recv()
            first[slot] = compute(slot)
            second[last] = pair_sum(last, first[last])
            last = slot
    second[last] = pair_sum(last, first[last])

    peak = jnp.full((half, 1), -jnp.inf, F32)
    norm = jnp.zeros((half, 1), F32)
    for slot in order:
        for copy in second[slot]:
            copy.wait_recv()
        logit = l2[slot]
        total = t2[slot].astype(F32)
        for r in range(m // 2 - 1):
            logit = logit + lx[slot, r]
            total = total + tx[slot, r].astype(F32)
        logit = jnp.where(key_pos(slot, half) <= half_pos, logit, -jnp.inf)
        lall[slot] = logit
        tall[slot] = total
        peak = jnp.maximum(peak, jnp.max(logit, axis=1, keepdims=True))
        norm = norm + jnp.sum(total, axis=1, keepdims=True)
    mass = jnp.zeros((half, 1), F32)
    for slot in order:
        expo = jnp.exp(lall[slot] - peak)
        lall[slot] = expo
        mass = mass + jnp.sum(expo, axis=1, keepdims=True)
    inv_mass = 1.0 / mass
    inv_norm = 1.0 / norm
    for slot in order:
        dbuf[c, slot] = (lall[slot] * inv_mass - tall[slot] * inv_norm).astype(BF16)
    swap = remote(dbuf.at[c], dbuf.at[c], d_send.at[0], d_recv.at[0], (s, partner))

    token = lax.broadcasted_iota(jnp.int32, (rows * iheads, rows), 0) // iheads
    spread = (token == lax.broadcasted_iota(jnp.int32, (rows * iheads, rows), 1)).astype(F32).astype(BF16)
    gwacc[...] = jnp.zeros_like(gwacc)
    swap.wait_recv()

    incoming = []
    own = None
    for slot in order[::-1]:
        delta = jnp.concatenate([dbuf[0, slot], dbuf[1, slot]], axis=0)
        wide = jnp.dot(spread, delta, preferred_element_type=F32)
        rectified = iscore[slot]
        gwacc[...] += wide * rectified
        part = jnp.where(rectified > 0, wide * wb[...], 0.0).astype(BF16)
        dall[:, slot * rows:(slot + 1) * rows] = part
        grad = lax.dot_general(part, qi_ref[...], (((0,), (0,)), ((), ())), preferred_element_type=F32)
        if slot == 0:
            own = grad
        else:
            gkbuf[slot - 1] = grad.astype(BF16)
            incoming.append((slot, remote(
                gkbuf.at[slot - 1], gkrecv.at[slot - 1], gk_send.at[slot - 1],
                gk_recv.at[slot - 1], (seq_off(offsets[slot]), h))))

    keys = kibuf[...].reshape(n * rows, ki_ref.shape[2])
    gq_ref[...] = jnp.dot(dall[...], keys, preferred_element_type=F32)
    wscore[...] = jnp.broadcast_to(jnp.sum(gwacc[...], axis=1, keepdims=True), wscore.shape)
    for g in range(iheads):
        gw_ref[:, g:g + 1] = wscore[pl.ds(g, rows, stride=iheads), :][:, 0:1]

    for slot, copy in incoming:
        copy.wait_recv()
        own = own + gkrecv[slot - 1].astype(F32)
    hbuf[h] = own.astype(BF16)
    swaps = []
    for r in range(1, m):
        peer = (h + r) % m
        swaps.append(remote(hbuf.at[h], hbuf.at[h], h_send.at[r - 1], h_recv.at[r - 1], (s, peer)))
    for copy in swaps:
        copy.wait_recv()
    result = hbuf[0].astype(F32)
    for r in range(1, m):
        result = result + hbuf[r].astype(F32)
    gk_ref[...] = result
    for copy in pending:
        copy.wait_send()


def solution(mesh):
    n, m = mesh.shape["seq"], mesh.shape["head"]

    def on_device(q_latent, kv_latent, normalizer, q_index, k_index, index_weight, span_pos):
        rows, heads, latent = q_latent.shape
        iheads, idim = q_index.shape[1:]
        half = rows // 2
        span = rows * n // span_pos.shape[0]
        peers = max(m // 2 - 1, 1)
        V = pltpu.VMEM
        D = pltpu.SemaphoreType.DMA
        scratch = [
            V((n, 2, half, latent), BF16), V((n, 2, half, idim), BF16),
            V((rows * heads, rows), F32), V((rows * iheads, rows), F32),
            V((rows * heads, rows), F32), V((rows * iheads, rows), F32),
            V((n, rows * iheads, rows), F32),
            V((n, 2, half, rows), F32), V((n, 2, half, rows), BF16),
            V((n, half, rows), F32), V((n, half, rows), BF16),
            V((n, half, rows), F32), V((n, half, rows), BF16),
            V((n, peers, half, rows), F32), V((n, peers, half, rows), BF16),
            V((n, half, rows), F32), V((n, half, rows), F32),
            V((2, n, half, rows), BF16), V((rows * iheads, n * rows), BF16),
            V((rows * iheads, rows), F32),
            V((n - 1, rows, idim), BF16), V((n - 1, rows, idim), BF16),
            V((m, rows, idim), BF16),
            D((n, 2)), D((n, 2)), D((n, 2)), D((n, 2)), D((n, 2)), D((n, 2)),
            D((n, peers, 2)), D((n, peers, 2)), D((1,)), D((1,)),
            D((n - 1,)), D((n - 1,)), D((m - 1,)), D((m - 1,)),
        ]
        vmem = pl.BlockSpec(memory_space=pltpu.VMEM)
        gq, gw, gk = pl.pallas_call(
            functools.partial(kernel, n, m, heads, iheads, span),
            out_shape=(
                jax.ShapeDtypeStruct((rows * iheads, idim), F32),
                jax.ShapeDtypeStruct((rows, iheads), F32),
                jax.ShapeDtypeStruct((rows, idim), F32),
            ),
            in_specs=[vmem] * 6 + [pl.BlockSpec(memory_space=pltpu.SMEM)],
            out_specs=(vmem, vmem, vmem),
            scratch_shapes=scratch,
            compiler_params=pltpu.CompilerParams(
                collective_id=0, has_side_effects=True, vmem_limit_bytes=60 * 2 ** 20
            ),
        )(
            q_latent.reshape(rows * heads, latent), kv_latent.reshape(2, half, latent),
            normalizer, q_index.reshape(rows * iheads, idim),
            k_index.reshape(2, half, idim), index_weight, span_pos,
        )
        return gq.reshape(rows, iheads, idim), gw, gk

    in_specs = (
        P("seq", "head", None), P("seq", None), P("seq", "head"), P("seq", "head", None),
        P("seq", None), P("seq", "head"), P(),
    )
    out_specs = (P("seq", "head", None), P("seq", "head"), P("seq", None))
    return jax.shard_map(
        on_device, mesh=mesh, in_specs=in_specs, out_specs=out_specs, check_vma=False
    )
```

```python
import functools

import jax
import jax.numpy as jnp
from jax import lax
from jax.experimental import pallas as pl
from jax.experimental.pallas import tpu as pltpu
from jax.sharding import PartitionSpec as P

MESH = pl.DeviceIdType.MESH
F32 = jnp.float32
BF16 = jnp.bfloat16
softmax_scale = 192.0 ** (-0.5)


def kernel(
    n, m, heads, iheads, span,
    q_ref, kv_ref, norm_ref, qi_ref, ki_ref, w_ref, span_ref,
    gq_ref, gw_ref, gk_ref,
    kvbuf, kibuf, qraw, qrows, normb, wb, attn, wscore, iscore, lbuf, tbuf, l1, t1, l2, t2, lx, tx,
    lall, tall, dbuf, dall, gwacc, gkbuf, gkrecv, hbuf,
    q_sem, ring_send, ring_recv, core_send, core_recv, s1_send, s1_recv, s2_send, s2_recv,
    d_send, d_recv, gk_send, gk_recv, h_send, h_recv,
):
    s = lax.axis_index("seq")
    h = lax.axis_index("head")
    rows = kv_ref.shape[2]
    half = rows // 2
    latent = 2 * kv_ref.shape[1]
    c = h % 2
    other = 1 - c
    partner = h + 1 - 2 * c
    near = n // 2

    def seq_at(pos):
        upper = pos // near
        return upper * (2 * (n - 1 - pos) + 1) + (1 - upper) * 2 * pos

    column = s % 2
    place = column * (n - 1 - s // 2) + (1 - column) * (s // 2)

    def seq_off(off):
        return seq_at((place + off + n) % n)

    loads = [pltpu.make_async_copy(q_ref.at[g], qraw.at[g], q_sem.at[g]) for g in range(heads)]
    for load in loads:
        load.start()
    barrier = pltpu.get_barrier_semaphore()
    for d in range(1, n):
        pl.semaphore_signal(barrier, inc=1, device_id=((s + d) % n, h), device_id_type=MESH)
    for d in range(1, m):
        pl.semaphore_signal(barrier, inc=1, device_id=(s, (h + d) % m), device_id_type=MESH)
    pl.semaphore_wait(barrier, n - 1 + m - 1)

    forward = n // 2
    backward = n - 1 - forward
    offsets = {0: 0}
    for k in range(1, forward + 1):
        offsets[k] = -k
    for k in range(1, backward + 1):
        offsets[forward + k] = k
    order = [0]
    for k in range(1, forward + 1):
        order.append(k)
        if k <= backward:
            order.append(forward + k)

    pending = []

    def remote(src, dst, send, recv, device):
        copy = pltpu.make_async_remote_copy(
            src_ref=src, dst_ref=dst, send_sem=send, recv_sem=recv,
            device_id=device, device_id_type=MESH,
        )
        copy.start()
        pending.append(copy)
        return copy

    def ring_copy(source, target, peer):
        if source == 0:
            kv_src, ki_src = kv_ref.at[c], ki_ref.at[c]
        else:
            kv_src, ki_src = kvbuf.at[source, c], kibuf.at[source, c]
        return (
            remote(kv_src, kvbuf.at[target, c], ring_send.at[target, 0],
                   ring_recv.at[target, 0], (peer, h)),
            remote(ki_src, kibuf.at[target, c], ring_send.at[target, 1],
                   ring_recv.at[target, 1], (peer, h)),
        )

    def core_copy(slot):
        return (
            remote(kvbuf.at[slot, c], kvbuf.at[slot, c], core_send.at[slot, 0],
                   core_recv.at[slot, 0], (s, partner)),
            remote(kibuf.at[slot, c], kibuf.at[slot, c], core_send.at[slot, 1],
                   core_recv.at[slot, 1], (s, partner)),
        )

    following, preceding = seq_off(1), seq_off(-1)
    ring = {1: ring_copy(0, 1, following)}
    if backward:
        ring[forward + 1] = ring_copy(0, forward + 1, preceding)
    kibuf[0] = ki_ref[...]

    for g in range(heads):
        normb[g * rows:(g + 1) * rows, :] = jnp.broadcast_to(norm_ref[g:g + 1, :], (rows, rows)).T
    for g in range(iheads):
        wb[pl.ds(g, rows, stride=iheads), :] = jnp.broadcast_to(w_ref[g:g + 1, :], (rows, rows)).T
    for g, load in enumerate(loads):
        load.wait()
        qrows[g * rows:(g + 1) * rows, :] = qraw[g].T

    per_block = rows // span

    def positions(block, index):
        found = jnp.zeros(index.shape, jnp.int32)
        for t in range(per_block):
            base = span_ref[block * per_block + t]
            found = jnp.where(index // span == t, base * span + index % span, found)
        return found

    query_pos = positions(s, lax.broadcasted_iota(jnp.int32, (rows, rows), 0))
    half_pos = positions(s, lax.broadcasted_iota(jnp.int32, (half, rows), 0) + c * half)

    def key_pos(slot, count):
        return positions(seq_off(offsets[slot]), lax.broadcasted_iota(jnp.int32, (count, rows), 1))

    contract_last = (((1,), (1,)), ((), ()))

    def compute(slots):
        width = len(slots) * rows
        kv = jnp.concatenate(
            [(kv_ref[...] if slot == 0 else kvbuf[slot]).reshape(latent, rows) for slot in slots], axis=1
        )
        scores = jnp.dot(qrows[...], kv, preferred_element_type=F32)
        attn[:, 0:width] = scores
        keys = jnp.concatenate([kibuf[slot].reshape(rows, ki_ref.shape[2]) for slot in slots], axis=0)
        raw_index = lax.dot_general(qi_ref[...], keys, contract_last, preferred_element_type=F32)
        out = {}
        for i, slot in enumerate(slots):
            lanes = slice(i * rows, (i + 1) * rows)
            rectified = jnp.maximum(raw_index[:, lanes], 0.0)
            iscore[slot] = rectified
            wscore[...] = wb[...] * rectified
            logit = wscore[pl.ds(0, rows, stride=iheads), :]
            for g in range(1, iheads):
                logit = logit + wscore[pl.ds(g, rows, stride=iheads), :]
            lbuf[slot] = logit.reshape(2, half, rows)
            total = jnp.zeros((rows, rows), F32)
            for g in range(heads):
                band = slice(g * rows, (g + 1) * rows)
                total = total + jnp.exp(attn[band, lanes] * softmax_scale - normb[band, :])
            total = jnp.where(key_pos(slot, rows) <= query_pos, total, 0.0).astype(BF16)
            tbuf[slot] = total.reshape(2, half, rows)
            out[slot] = (
                remote(lbuf.at[slot, other], l1.at[slot], s1_send.at[slot, 0],
                       s1_recv.at[slot, 0], (s, partner)),
                remote(tbuf.at[slot, other], t1.at[slot], s1_send.at[slot, 1],
                       s1_recv.at[slot, 1], (s, partner)),
            )
        return out

    def pair_sum(slot, copies):
        for copy in copies:
            copy.wait_recv()
        l2[slot] = lbuf[slot, c] + l1[slot]
        t2[slot] = (tbuf[slot, c].astype(F32) + t1[slot].astype(F32)).astype(BF16)
        out = []
        for r in range(1, m // 2):
            peer = (h + 2 * r) % m
            out.append(remote(l2.at[slot], lx.at[slot, r - 1], s2_send.at[slot, r - 1, 0],
                              s2_recv.at[slot, r - 1, 0], (s, peer)))
            out.append(remote(t2.at[slot], tx.at[slot, r - 1], s2_send.at[slot, r - 1, 1],
                              s2_recv.at[slot, r - 1, 1], (s, peer)))
        return out

    first = compute([0])
    second = {}
    waiting = [0]
    for k in range(1, forward + 1):
        arrived = [k] + ([forward + k] if k <= backward else [])
        core = {}
        for slot in arrived:
            for copy in ring[slot]:
                copy.wait_recv()
            if slot <= forward and k < forward:
                ring[slot + 1] = ring_copy(slot, slot + 1, following)
            if slot > forward and k < backward:
                ring[slot + 1] = ring_copy(slot, slot + 1, preceding)
            core[slot] = core_copy(slot)
        for slot in waiting:
            second[slot] = pair_sum(slot, first[slot])
        for slot in arrived:
            for copy in core[slot]:
                copy.wait_recv()
        first.update(compute(arrived))
        waiting = arrived
    for slot in waiting:
        second[slot] = pair_sum(slot, first[slot])

    peak = jnp.full((half, 1), -jnp.inf, F32)
    norm = jnp.zeros((half, 1), F32)
    for slot in order:
        for copy in second[slot]:
            copy.wait_recv()
        logit = l2[slot]
        total = t2[slot].astype(F32)
        for r in range(m // 2 - 1):
            logit = logit + lx[slot, r]
            total = total + tx[slot, r].astype(F32)
        logit = jnp.where(key_pos(slot, half) <= half_pos, logit, -jnp.inf)
        lall[slot] = logit
        tall[slot] = total
        peak = jnp.maximum(peak, jnp.max(logit, axis=1, keepdims=True))
        norm = norm + jnp.sum(total, axis=1, keepdims=True)
    mass = jnp.zeros((half, 1), F32)
    for slot in order:
        expo = jnp.exp(lall[slot] - peak)
        lall[slot] = expo
        mass = mass + jnp.sum(expo, axis=1, keepdims=True)
    inv_mass = 1.0 / mass
    inv_norm = 1.0 / norm
    for slot in order:
        dbuf[c, slot] = (lall[slot] * inv_mass - tall[slot] * inv_norm).astype(BF16)
    swap = remote(dbuf.at[c], dbuf.at[c], d_send.at[0], d_recv.at[0], (s, partner))

    token = lax.broadcasted_iota(jnp.int32, (rows * iheads, rows), 0) // iheads
    spread = (token == lax.broadcasted_iota(jnp.int32, (rows * iheads, rows), 1)).astype(F32).astype(BF16)
    gwacc[...] = jnp.zeros_like(gwacc)
    swap.wait_recv()

    incoming = []
    own = None
    for slot in order[::-1]:
        delta = jnp.concatenate([dbuf[0, slot], dbuf[1, slot]], axis=0)
        wide = jnp.dot(spread, delta, preferred_element_type=F32)
        rectified = iscore[slot]
        gwacc[...] += wide * rectified
        part = jnp.where(rectified > 0, wide * wb[...], 0.0).astype(BF16)
        dall[:, slot * rows:(slot + 1) * rows] = part
        grad = lax.dot_general(part, qi_ref[...], (((0,), (0,)), ((), ())), preferred_element_type=F32)
        if slot == 0:
            own = grad
        else:
            gkbuf[slot - 1] = grad.astype(BF16)
            incoming.append((slot, remote(
                gkbuf.at[slot - 1], gkrecv.at[slot - 1], gk_send.at[slot - 1],
                gk_recv.at[slot - 1], (seq_off(offsets[slot]), h))))

    keys = kibuf[...].reshape(n * rows, ki_ref.shape[2])
    gq_ref[...] = jnp.dot(dall[...], keys, preferred_element_type=F32)
    for g in range(iheads):
        gw_ref[g:g + 1, :] = jnp.sum(gwacc[pl.ds(g, rows, stride=iheads), :].T, axis=0, keepdims=True)

    for slot, copy in incoming:
        copy.wait_recv()
        own = own + gkrecv[slot - 1].astype(F32)
    hbuf[h] = own.astype(BF16)
    swaps = []
    for r in range(1, m):
        peer = (h + r) % m
        swaps.append(remote(hbuf.at[h], hbuf.at[h], h_send.at[r - 1], h_recv.at[r - 1], (s, peer)))
    for copy in swaps:
        copy.wait_recv()
    result = hbuf[0].astype(F32)
    for r in range(1, m):
        result = result + hbuf[r].astype(F32)
    gk_ref[...] = result
    for copy in pending:
        copy.wait_send()


def solution(mesh):
    n, m = mesh.shape["seq"], mesh.shape["head"]

    def on_device(q_latent, kv_latent, normalizer, q_index, k_index, index_weight, span_pos):
        rows, heads, latent = q_latent.shape
        iheads, idim = q_index.shape[1:]
        half = rows // 2
        span = rows * n // span_pos.shape[0]
        peers = max(m // 2 - 1, 1)
        V = pltpu.VMEM
        D = pltpu.SemaphoreType.DMA
        scratch = [
            V((n, 2, latent // 2, rows), BF16), V((n, 2, half, idim), BF16),
            V((heads, latent, rows), BF16), V((rows * heads, latent), BF16),
            V((rows * heads, rows), F32), V((rows * iheads, rows), F32),
            V((rows * heads, 2 * rows), F32), V((rows * iheads, rows), F32),
            V((n, rows * iheads, rows), F32),
            V((n, 2, half, rows), F32), V((n, 2, half, rows), BF16),
            V((n, half, rows), F32), V((n, half, rows), BF16),
            V((n, half, rows), F32), V((n, half, rows), BF16),
            V((n, peers, half, rows), F32), V((n, peers, half, rows), BF16),
            V((n, half, rows), F32), V((n, half, rows), F32),
            V((2, n, half, rows), BF16), V((rows * iheads, n * rows), BF16),
            V((rows * iheads, rows), F32),
            V((n - 1, rows, idim), BF16), V((n - 1, rows, idim), BF16),
            V((m, rows, idim), BF16),
            D((heads,)), D((n, 2)), D((n, 2)), D((n, 2)), D((n, 2)), D((n, 2)), D((n, 2)),
            D((n, peers, 2)), D((n, peers, 2)), D((1,)), D((1,)),
            D((n - 1,)), D((n - 1,)), D((m - 1,)), D((m - 1,)),
        ]
        vmem = pl.BlockSpec(memory_space=pltpu.VMEM)
        gq, gw, gk = pl.pallas_call(
            functools.partial(kernel, n, m, heads, iheads, span),
            out_shape=(
                jax.ShapeDtypeStruct((rows * iheads, idim), F32),
                jax.ShapeDtypeStruct((iheads, rows), F32),
                jax.ShapeDtypeStruct((rows, idim), F32),
            ),
            in_specs=[pl.BlockSpec(memory_space=pl.ANY)] + [vmem] * 5 + [pl.BlockSpec(memory_space=pltpu.SMEM)],
            out_specs=(vmem, vmem, vmem),
            scratch_shapes=scratch,
            compiler_params=pltpu.CompilerParams(
                collective_id=0, has_side_effects=True, vmem_limit_bytes=60 * 2 ** 20
            ),
        )(
            q_latent.transpose(1, 2, 0), kv_latent.T.reshape(2, latent // 2, rows),
            normalizer.T, q_index.reshape(rows * iheads, idim),
            k_index.reshape(2, half, idim), index_weight.T, span_pos,
        )
        return gq.reshape(rows, iheads, idim), gw.T, gk

    in_specs = (
        P("seq", "head", None), P("seq", None), P("seq", "head"), P("seq", "head", None),
        P("seq", None), P("seq", "head"), P(),
    )
    out_specs = (P("seq", "head", None), P("seq", "head"), P("seq", None))
    return jax.shard_map(
        on_device, mesh=mesh, in_specs=in_specs, out_specs=out_specs, check_vma=False
    )
```

```python
import functools

import jax
import jax.numpy as jnp
from jax import lax
from jax.experimental import pallas as pl
from jax.experimental.pallas import tpu as pltpu
from jax.sharding import PartitionSpec as P

MESH = pl.DeviceIdType.MESH
F32 = jnp.float32
BF16 = jnp.bfloat16
softmax_scale = 192.0 ** (-0.5)


def kernel(
    n, m, heads, iheads, span, pieces,
    q_ref, kv_ref, norm_ref, qi_ref, ki_ref, w_ref, span_ref,
    gq_ref, gw_ref, gk_ref,
    kvbuf, kibuf, qraw, qrows, normb, wb, attn, wscore, iscore, lbuf, tbuf, l1, t1, l2, t2, lx, tx,
    lall, tall, dbuf, dall, gwacc, gkbuf, gkrecv, hbuf,
    q_sem, ring_send, ring_recv, core_send, core_recv, s1_send, s1_recv, s2_send, s2_recv,
    d_send, d_recv, gk_send, gk_recv, h_send, h_recv,
):
    s = lax.axis_index("seq")
    h = lax.axis_index("head")
    rows = kv_ref.shape[2]
    half = rows // 2
    latent = 2 * kv_ref.shape[1]
    depth = kv_ref.shape[1] // pieces
    c = h % 2
    other = 1 - c
    partner = h + 1 - 2 * c
    near = n // 2

    def seq_at(pos):
        upper = pos // near
        return upper * (2 * (n - 1 - pos) + 1) + (1 - upper) * 2 * pos

    column = s % 2
    place = column * (n - 1 - s // 2) + (1 - column) * (s // 2)

    def seq_off(off):
        return seq_at((place + off + n) % n)

    loads = [pltpu.make_async_copy(q_ref.at[g], qraw.at[g], q_sem.at[g]) for g in range(heads)]
    for load in loads:
        load.start()
    barrier = pltpu.get_barrier_semaphore()
    for d in range(1, n):
        pl.semaphore_signal(barrier, inc=1, device_id=((s + d) % n, h), device_id_type=MESH)
    for d in range(1, m):
        pl.semaphore_signal(barrier, inc=1, device_id=(s, (h + d) % m), device_id_type=MESH)
    pl.semaphore_wait(barrier, n - 1 + m - 1)

    forward = n // 2
    backward = n - 1 - forward
    offsets = {0: 0}
    for k in range(1, forward + 1):
        offsets[k] = -k
    for k in range(1, backward + 1):
        offsets[forward + k] = k
    order = [0]
    for k in range(1, forward + 1):
        order.append(k)
        if k <= backward:
            order.append(forward + k)

    pending = []

    def remote(src, dst, send, recv, device):
        copy = pltpu.make_async_remote_copy(
            src_ref=src, dst_ref=dst, send_sem=send, recv_sem=recv,
            device_id=device, device_id_type=MESH,
        )
        copy.start()
        pending.append(copy)
        return copy

    def view(kv, ki, piece):
        if piece == pieces:
            return ki
        return kv.at[pl.ds(piece * depth, depth)]

    def ring_copy(source, target, peer, piece):
        if source == 0:
            src = view(kv_ref.at[c], ki_ref.at[c], piece)
        else:
            src = view(kvbuf.at[source, c], kibuf.at[source, c], piece)
        return remote(src, view(kvbuf.at[target, c], kibuf.at[target, c], piece),
                      ring_send.at[target, piece], ring_recv.at[target, piece], (peer, h))

    def core_copy(slot, piece):
        block = view(kvbuf.at[slot, c], kibuf.at[slot, c], piece)
        return remote(block, block, core_send.at[slot, piece], core_recv.at[slot, piece], (s, partner))

    following, preceding = seq_off(1), seq_off(-1)
    ring = {}
    for piece in range(pieces + 1):
        ring[1, piece] = ring_copy(0, 1, following, piece)
        if backward:
            ring[forward + 1, piece] = ring_copy(0, forward + 1, preceding, piece)
    kibuf[0] = ki_ref[...]

    for g in range(heads):
        normb[g * rows:(g + 1) * rows, :] = jnp.broadcast_to(norm_ref[g:g + 1, :], (rows, rows)).T
    for g in range(iheads):
        wb[pl.ds(g, rows, stride=iheads), :] = jnp.broadcast_to(w_ref[g:g + 1, :], (rows, rows)).T
    for g, load in enumerate(loads):
        load.wait()
        qrows[g * rows:(g + 1) * rows, :] = qraw[g].T

    per_block = rows // span

    def positions(block, index):
        found = jnp.zeros(index.shape, jnp.int32)
        for t in range(per_block):
            base = span_ref[block * per_block + t]
            found = jnp.where(index // span == t, base * span + index % span, found)
        return found

    query_pos = positions(s, lax.broadcasted_iota(jnp.int32, (rows, rows), 0))
    half_pos = positions(s, lax.broadcasted_iota(jnp.int32, (half, rows), 0) + c * half)

    def key_pos(slot, count):
        return positions(seq_off(offsets[slot]), lax.broadcasted_iota(jnp.int32, (count, rows), 1))

    contract_last = (((1,), (1,)), ((), ()))

    def compute(slots):
        width = len(slots) * rows
        kv = jnp.concatenate(
            [(kv_ref[...] if slot == 0 else kvbuf[slot]).reshape(latent, rows) for slot in slots], axis=1
        )
        scores = jnp.dot(qrows[...], kv, preferred_element_type=F32)
        attn[:, 0:width] = scores
        keys = jnp.concatenate([kibuf[slot].reshape(rows, ki_ref.shape[2]) for slot in slots], axis=0)
        raw_index = lax.dot_general(qi_ref[...], keys, contract_last, preferred_element_type=F32)
        out = {}
        for i, slot in enumerate(slots):
            lanes = slice(i * rows, (i + 1) * rows)
            rectified = jnp.maximum(raw_index[:, lanes], 0.0)
            iscore[slot] = rectified
            wscore[...] = wb[...] * rectified
            logit = wscore[pl.ds(0, rows, stride=iheads), :]
            for g in range(1, iheads):
                logit = logit + wscore[pl.ds(g, rows, stride=iheads), :]
            lbuf[slot] = logit.reshape(2, half, rows)
            total = jnp.zeros((rows, rows), F32)
            for g in range(heads):
                band = slice(g * rows, (g + 1) * rows)
                total = total + jnp.exp(attn[band, lanes] * softmax_scale - normb[band, :])
            total = jnp.where(key_pos(slot, rows) <= query_pos, total, 0.0).astype(BF16)
            tbuf[slot] = total.reshape(2, half, rows)
            out[slot] = (
                remote(lbuf.at[slot, other], l1.at[slot], s1_send.at[slot, 0],
                       s1_recv.at[slot, 0], (s, partner)),
                remote(tbuf.at[slot, other], t1.at[slot], s1_send.at[slot, 1],
                       s1_recv.at[slot, 1], (s, partner)),
            )
        return out

    def pair_sum(slot, copies):
        for copy in copies:
            copy.wait_recv()
        l2[slot] = lbuf[slot, c] + l1[slot]
        t2[slot] = (tbuf[slot, c].astype(F32) + t1[slot].astype(F32)).astype(BF16)
        out = []
        for r in range(1, m // 2):
            peer = (h + 2 * r) % m
            out.append(remote(l2.at[slot], lx.at[slot, r - 1], s2_send.at[slot, r - 1, 0],
                              s2_recv.at[slot, r - 1, 0], (s, peer)))
            out.append(remote(t2.at[slot], tx.at[slot, r - 1], s2_send.at[slot, r - 1, 1],
                              s2_recv.at[slot, r - 1, 1], (s, peer)))
        return out

    first = compute([0])
    second = {}
    waiting = [0]
    for k in range(1, forward + 1):
        arrived = [k] + ([forward + k] if k <= backward else [])
        core = {}
        for piece in range(pieces + 1):
            for slot in arrived:
                ring[slot, piece].wait_recv()
                if slot <= forward and k < forward:
                    ring[slot + 1, piece] = ring_copy(slot, slot + 1, following, piece)
                if slot > forward and k < backward:
                    ring[slot + 1, piece] = ring_copy(slot, slot + 1, preceding, piece)
                core[slot, piece] = core_copy(slot, piece)
        for slot in waiting:
            second[slot] = pair_sum(slot, first[slot])
        for slot in arrived:
            for piece in range(pieces + 1):
                core[slot, piece].wait_recv()
        first.update(compute(arrived))
        waiting = arrived
    for slot in waiting:
        second[slot] = pair_sum(slot, first[slot])

    peak = jnp.full((half, 1), -jnp.inf, F32)
    norm = jnp.zeros((half, 1), F32)
    for slot in order:
        for copy in second[slot]:
            copy.wait_recv()
        logit = l2[slot]
        total = t2[slot].astype(F32)
        for r in range(m // 2 - 1):
            logit = logit + lx[slot, r]
            total = total + tx[slot, r].astype(F32)
        logit = jnp.where(key_pos(slot, half) <= half_pos, logit, -jnp.inf)
        lall[slot] = logit
        tall[slot] = total
        peak = jnp.maximum(peak, jnp.max(logit, axis=1, keepdims=True))
        norm = norm + jnp.sum(total, axis=1, keepdims=True)
    mass = jnp.zeros((half, 1), F32)
    for slot in order:
        expo = jnp.exp(lall[slot] - peak)
        lall[slot] = expo
        mass = mass + jnp.sum(expo, axis=1, keepdims=True)
    inv_mass = 1.0 / mass
    inv_norm = 1.0 / norm
    for slot in order:
        dbuf[c, slot] = (lall[slot] * inv_mass - tall[slot] * inv_norm).astype(BF16)
    swap = remote(dbuf.at[c], dbuf.at[c], d_send.at[0], d_recv.at[0], (s, partner))

    token = lax.broadcasted_iota(jnp.int32, (rows * iheads, rows), 0) // iheads
    spread = (token == lax.broadcasted_iota(jnp.int32, (rows * iheads, rows), 1)).astype(F32).astype(BF16)
    gwacc[...] = jnp.zeros_like(gwacc)
    swap.wait_recv()

    incoming = []
    own = None
    for slot in order[::-1]:
        delta = jnp.concatenate([dbuf[0, slot], dbuf[1, slot]], axis=0)
        wide = jnp.dot(spread, delta, preferred_element_type=F32)
        rectified = iscore[slot]
        gwacc[...] += wide * rectified
        part = jnp.where(rectified > 0, wide * wb[...], 0.0).astype(BF16)
        dall[:, slot * rows:(slot + 1) * rows] = part
        grad = lax.dot_general(part, qi_ref[...], (((0,), (0,)), ((), ())), preferred_element_type=F32)
        if slot == 0:
            own = grad
        else:
            gkbuf[slot - 1] = grad.astype(BF16)
            incoming.append((slot, remote(
                gkbuf.at[slot - 1], gkrecv.at[slot - 1], gk_send.at[slot - 1],
                gk_recv.at[slot - 1], (seq_off(offsets[slot]), h))))

    keys = kibuf[...].reshape(n * rows, ki_ref.shape[2])
    gq_ref[...] = jnp.dot(dall[...], keys, preferred_element_type=F32)
    for g in range(iheads):
        gw_ref[g:g + 1, :] = jnp.sum(gwacc[pl.ds(g, rows, stride=iheads), :].T, axis=0, keepdims=True)

    for slot, copy in incoming:
        copy.wait_recv()
        own = own + gkrecv[slot - 1].astype(F32)
    hbuf[h] = own.astype(BF16)
    swaps = []
    for r in range(1, m):
        peer = (h + r) % m
        swaps.append(remote(hbuf.at[h], hbuf.at[h], h_send.at[r - 1], h_recv.at[r - 1], (s, peer)))
    for copy in swaps:
        copy.wait_recv()
    result = hbuf[0].astype(F32)
    for r in range(1, m):
        result = result + hbuf[r].astype(F32)
    gk_ref[...] = result
    for copy in pending:
        copy.wait_send()


def write_out(gq_in, gw_in, gk_in, gq_ref, gw_ref, gk_ref):
    gq_ref[...] = gq_in[...]
    gw_ref[...] = gw_in[...]
    gk_ref[...] = gk_in[...]


def solution(mesh):
    n, m = mesh.shape["seq"], mesh.shape["head"]

    def on_device(q_latent, kv_latent, normalizer, q_index, k_index, index_weight, span_pos):
        rows, heads, latent = q_latent.shape
        iheads, idim = q_index.shape[1:]
        half = rows // 2
        span = rows * n // span_pos.shape[0]
        pieces = 3 if latent % 96 == 0 else 1
        peers = max(m // 2 - 1, 1)
        V = pltpu.VMEM
        D = pltpu.SemaphoreType.DMA
        scratch = [
            V((n, 2, latent // 2, rows), BF16), V((n, 2, half, idim), BF16),
            V((heads, latent, rows), BF16), V((rows * heads, latent), BF16),
            V((rows * heads, rows), F32), V((rows * iheads, rows), F32),
            V((rows * heads, 2 * rows), F32), V((rows * iheads, rows), F32),
            V((n, rows * iheads, rows), F32),
            V((n, 2, half, rows), F32), V((n, 2, half, rows), BF16),
            V((n, half, rows), F32), V((n, half, rows), BF16),
            V((n, half, rows), F32), V((n, half, rows), BF16),
            V((n, peers, half, rows), F32), V((n, peers, half, rows), BF16),
            V((n, half, rows), F32), V((n, half, rows), F32),
            V((2, n, half, rows), BF16), V((rows * iheads, n * rows), BF16),
            V((rows * iheads, rows), F32),
            V((n - 1, rows, idim), BF16), V((n - 1, rows, idim), BF16),
            V((m, rows, idim), BF16),
            D((heads,)), D((n, pieces + 1)), D((n, pieces + 1)), D((n, pieces + 1)),
            D((n, pieces + 1)), D((n, 2)), D((n, 2)),
            D((n, peers, 2)), D((n, peers, 2)), D((1,)), D((1,)),
            D((n - 1,)), D((n - 1,)), D((m - 1,)), D((m - 1,)),
        ]
        vmem = pl.BlockSpec(memory_space=pltpu.VMEM)
        results = pl.pallas_call(
            functools.partial(kernel, n, m, heads, iheads, span, pieces),
            out_shape=(
                jax.ShapeDtypeStruct((rows * iheads, idim), F32),
                jax.ShapeDtypeStruct((iheads, rows), F32),
                jax.ShapeDtypeStruct((rows, idim), F32),
            ),
            in_specs=[pl.BlockSpec(memory_space=pl.ANY)] + [vmem] * 5 + [pl.BlockSpec(memory_space=pltpu.SMEM)],
            out_specs=(vmem, vmem, vmem),
            scratch_shapes=scratch,
            compiler_params=pltpu.CompilerParams(
                collective_id=0, has_side_effects=True, vmem_limit_bytes=60 * 2 ** 20
            ),
        )(
            q_latent.transpose(1, 2, 0), kv_latent.T.reshape(2, latent // 2, rows),
            normalizer.T, q_index.reshape(rows * iheads, idim),
            k_index.reshape(2, half, idim), index_weight.T, span_pos,
        )
        gq, gw, gk = pl.pallas_call(
            write_out,
            out_shape=tuple(jax.ShapeDtypeStruct(x.shape, x.dtype) for x in results),
            in_specs=[vmem] * 3,
            out_specs=(vmem,) * 3,
        )(*results)
        return gq.reshape(rows, iheads, idim), gw.T, gk

    in_specs = (
        P("seq", "head", None), P("seq", None), P("seq", "head"), P("seq", "head", None),
        P("seq", None), P("seq", "head"), P(),
    )
    out_specs = (P("seq", "head", None), P("seq", "head"), P("seq", None))
    return jax.shard_map(
        on_device, mesh=mesh, in_specs=in_specs, out_specs=out_specs, check_vma=False
    )
```

```python
import functools

import jax
import jax.numpy as jnp
from jax import lax
from jax.experimental import pallas as pl
from jax.experimental.pallas import tpu as pltpu
from jax.sharding import PartitionSpec as P

MESH = pl.DeviceIdType.MESH
F32 = jnp.float32
BF16 = jnp.bfloat16
softmax_scale = 192.0 ** (-0.5)


def kernel(
    n, m, heads, iheads, span, pieces,
    q_ref, kv_ref, norm_ref, qi_ref, ki_ref, w_ref, span_ref,
    gq_ref, gw_ref, gk_ref,
    kvbuf, kibuf, qraw, qrows, normb, wb, attn, wscore, iscore, lbuf, tbuf, l1, t1, l2, t2, lx, tx,
    lall, tall, dbuf, dall, gwacc, gkbuf, gkpair, gksum, gkrecv, hbuf,
    q_sem, ring_send, ring_recv, core_send, core_recv, s1_send, s1_recv, s2_send, s2_recv,
    d_send, d_recv, gp_send, gp_recv, gk_send, gk_recv, h_send, h_recv,
):
    s = lax.axis_index("seq")
    h = lax.axis_index("head")
    rows = kv_ref.shape[2]
    half = rows // 2
    latent = 2 * kv_ref.shape[1]
    depth = kv_ref.shape[1] // pieces
    c = h % 2
    other = 1 - c
    partner = h + 1 - 2 * c
    near = n // 2

    def seq_at(pos):
        upper = pos // near
        return upper * (2 * (n - 1 - pos) + 1) + (1 - upper) * 2 * pos

    column = s % 2
    place = column * (n - 1 - s // 2) + (1 - column) * (s // 2)

    def seq_off(off):
        return seq_at((place + off + n) % n)

    loads = [pltpu.make_async_copy(q_ref.at[g], qraw.at[g], q_sem.at[g]) for g in range(heads)]
    for load in loads:
        load.start()
    barrier = pltpu.get_barrier_semaphore()
    for d in range(1, n):
        pl.semaphore_signal(barrier, inc=1, device_id=((s + d) % n, h), device_id_type=MESH)
    for d in range(1, m):
        pl.semaphore_signal(barrier, inc=1, device_id=(s, (h + d) % m), device_id_type=MESH)
    pl.semaphore_wait(barrier, n - 1 + m - 1)

    forward = n // 2
    backward = n - 1 - forward
    offsets = {0: 0}
    for k in range(1, forward + 1):
        offsets[k] = -k
    for k in range(1, backward + 1):
        offsets[forward + k] = k
    order = [0]
    for k in range(1, forward + 1):
        order.append(k)
        if k <= backward:
            order.append(forward + k)

    pending = []

    def remote(src, dst, send, recv, device):
        copy = pltpu.make_async_remote_copy(
            src_ref=src, dst_ref=dst, send_sem=send, recv_sem=recv,
            device_id=device, device_id_type=MESH,
        )
        copy.start()
        pending.append(copy)
        return copy

    def view(kv, ki, piece):
        if piece == pieces:
            return ki
        return kv.at[pl.ds(piece * depth, depth)]

    def ring_copy(source, target, peer, piece):
        if source == 0:
            src = view(kv_ref.at[c], ki_ref.at[c], piece)
        else:
            src = view(kvbuf.at[source, c], kibuf.at[source, c], piece)
        return remote(src, view(kvbuf.at[target, c], kibuf.at[target, c], piece),
                      ring_send.at[target, piece], ring_recv.at[target, piece], (peer, h))

    def core_copy(slot, piece):
        block = view(kvbuf.at[slot, c], kibuf.at[slot, c], piece)
        return remote(block, block, core_send.at[slot, piece], core_recv.at[slot, piece], (s, partner))

    following, preceding = seq_off(1), seq_off(-1)
    ring = {}
    for piece in range(pieces + 1):
        ring[1, piece] = ring_copy(0, 1, following, piece)
        if backward:
            ring[forward + 1, piece] = ring_copy(0, forward + 1, preceding, piece)
    kibuf[0] = ki_ref[...]

    for g in range(heads):
        normb[g * rows:(g + 1) * rows, :] = jnp.broadcast_to(norm_ref[g:g + 1, :], (rows, rows)).T
    for g in range(iheads):
        wb[pl.ds(g, rows, stride=iheads), :] = jnp.broadcast_to(w_ref[g:g + 1, :], (rows, rows)).T
    for g, load in enumerate(loads):
        load.wait()
        qrows[g * rows:(g + 1) * rows, :] = qraw[g].T

    per_block = rows // span

    def positions(block, index):
        found = jnp.zeros(index.shape, jnp.int32)
        for t in range(per_block):
            base = span_ref[block * per_block + t]
            found = jnp.where(index // span == t, base * span + index % span, found)
        return found

    query_pos = positions(s, lax.broadcasted_iota(jnp.int32, (rows, rows), 0))
    half_pos = positions(s, lax.broadcasted_iota(jnp.int32, (half, rows), 0) + c * half)

    def key_pos(slot, count):
        return positions(seq_off(offsets[slot]), lax.broadcasted_iota(jnp.int32, (count, rows), 1))

    contract_last = (((1,), (1,)), ((), ()))

    def compute(slots):
        width = len(slots) * rows
        kv = jnp.concatenate(
            [(kv_ref[...] if slot == 0 else kvbuf[slot]).reshape(latent, rows) for slot in slots], axis=1
        )
        scores = jnp.dot(qrows[...], kv, preferred_element_type=F32)
        attn[:, 0:width] = scores
        keys = jnp.concatenate([kibuf[slot].reshape(rows, ki_ref.shape[2]) for slot in slots], axis=0)
        raw_index = lax.dot_general(qi_ref[...], keys, contract_last, preferred_element_type=F32)
        out = {}
        for i, slot in enumerate(slots):
            lanes = slice(i * rows, (i + 1) * rows)
            rectified = jnp.maximum(raw_index[:, lanes], 0.0)
            iscore[slot] = rectified
            wscore[...] = wb[...] * rectified
            logit = wscore[pl.ds(0, rows, stride=iheads), :]
            for g in range(1, iheads):
                logit = logit + wscore[pl.ds(g, rows, stride=iheads), :]
            lbuf[slot] = logit.reshape(2, half, rows)
            total = jnp.zeros((rows, rows), F32)
            for g in range(heads):
                band = slice(g * rows, (g + 1) * rows)
                total = total + jnp.exp(attn[band, lanes] * softmax_scale - normb[band, :])
            total = jnp.where(key_pos(slot, rows) <= query_pos, total, 0.0).astype(BF16)
            tbuf[slot] = total.reshape(2, half, rows)
            out[slot] = (
                remote(lbuf.at[slot, other], l1.at[slot], s1_send.at[slot, 0],
                       s1_recv.at[slot, 0], (s, partner)),
                remote(tbuf.at[slot, other], t1.at[slot], s1_send.at[slot, 1],
                       s1_recv.at[slot, 1], (s, partner)),
            )
        return out

    def pair_sum(slot, copies):
        for copy in copies:
            copy.wait_recv()
        l2[slot] = lbuf[slot, c] + l1[slot]
        t2[slot] = (tbuf[slot, c].astype(F32) + t1[slot].astype(F32)).astype(BF16)
        out = []
        for r in range(1, m // 2):
            peer = (h + 2 * r) % m
            out.append(remote(l2.at[slot], lx.at[slot, r - 1], s2_send.at[slot, r - 1, 0],
                              s2_recv.at[slot, r - 1, 0], (s, peer)))
            out.append(remote(t2.at[slot], tx.at[slot, r - 1], s2_send.at[slot, r - 1, 1],
                              s2_recv.at[slot, r - 1, 1], (s, peer)))
        return out

    first = compute([0])
    second = {}
    waiting = [0]
    for k in range(1, forward + 1):
        arrived = [k] + ([forward + k] if k <= backward else [])
        core = {}
        for piece in range(pieces + 1):
            for slot in arrived:
                ring[slot, piece].wait_recv()
                if slot <= forward and k < forward:
                    ring[slot + 1, piece] = ring_copy(slot, slot + 1, following, piece)
                if slot > forward and k < backward:
                    ring[slot + 1, piece] = ring_copy(slot, slot + 1, preceding, piece)
                core[slot, piece] = core_copy(slot, piece)
        for slot in waiting:
            second[slot] = pair_sum(slot, first[slot])
        for slot in arrived:
            for piece in range(pieces + 1):
                core[slot, piece].wait_recv()
        first.update(compute(arrived))
        waiting = arrived
    for slot in waiting:
        second[slot] = pair_sum(slot, first[slot])

    peak = jnp.full((half, 1), -jnp.inf, F32)
    norm = jnp.zeros((half, 1), F32)
    for slot in order:
        for copy in second[slot]:
            copy.wait_recv()
        logit = l2[slot]
        total = t2[slot].astype(F32)
        for r in range(m // 2 - 1):
            logit = logit + lx[slot, r]
            total = total + tx[slot, r].astype(F32)
        logit = jnp.where(key_pos(slot, half) <= half_pos, logit, -jnp.inf)
        lall[slot] = logit
        tall[slot] = total
        peak = jnp.maximum(peak, jnp.max(logit, axis=1, keepdims=True))
        norm = norm + jnp.sum(total, axis=1, keepdims=True)
    mass = jnp.zeros((half, 1), F32)
    for slot in order:
        expo = jnp.exp(lall[slot] - peak)
        lall[slot] = expo
        mass = mass + jnp.sum(expo, axis=1, keepdims=True)
    inv_mass = 1.0 / mass
    inv_norm = 1.0 / norm
    for slot in order:
        dbuf[c, slot] = (lall[slot] * inv_mass - tall[slot] * inv_norm).astype(BF16)
    swap = remote(dbuf.at[c], dbuf.at[c], d_send.at[0], d_recv.at[0], (s, partner))

    token = lax.broadcasted_iota(jnp.int32, (rows * iheads, rows), 0) // iheads
    spread = (token == lax.broadcasted_iota(jnp.int32, (rows * iheads, rows), 1)).astype(F32).astype(BF16)
    gwacc[...] = jnp.zeros_like(gwacc)
    swap.wait_recv()

    incoming = []
    sums = []

    def pass_on(slot, copy):
        copy.wait_recv()
        pair = gkbuf[slot, c].astype(F32) + gkpair[slot].astype(F32)
        if slot == 0:
            return pair
        gksum[slot - 1] = pair.astype(BF16)
        incoming.append((slot, remote(
            gksum.at[slot - 1], gkrecv.at[slot - 1], gk_send.at[slot - 1],
            gk_recv.at[slot - 1], (seq_off(offsets[slot]), h))))
        return None

    for slot in order[::-1]:
        delta = jnp.concatenate([dbuf[0, slot], dbuf[1, slot]], axis=0)
        wide = jnp.dot(spread, delta, preferred_element_type=F32)
        rectified = iscore[slot]
        gwacc[...] += wide * rectified
        part = jnp.where(rectified > 0, wide * wb[...], 0.0).astype(BF16)
        dall[:, slot * rows:(slot + 1) * rows] = part
        grad = lax.dot_general(part, qi_ref[...], (((0,), (0,)), ((), ())), preferred_element_type=F32)
        gkbuf[slot] = grad.astype(BF16).reshape(2, half, grad.shape[1])
        sums.append((slot, remote(gkbuf.at[slot, other], gkpair.at[slot], gp_send.at[slot],
                                  gp_recv.at[slot], (s, partner))))
        if len(sums) > 3:
            pass_on(*sums.pop(0))
    for slot, copy in sums:
        own = pass_on(slot, copy)

    keys = kibuf[...].reshape(n * rows, ki_ref.shape[2])
    gq_ref[...] = jnp.dot(dall[...], keys, preferred_element_type=F32)
    for g in range(iheads):
        gw_ref[g:g + 1, :] = jnp.sum(gwacc[pl.ds(g, rows, stride=iheads), :].T, axis=0, keepdims=True)

    for slot, copy in incoming:
        copy.wait_recv()
        own = own + gkrecv[slot - 1].astype(F32)
    hbuf[h // 2, c] = own.astype(BF16)
    swaps = []
    for r in range(1, m):
        peer = (h + r) % m
        swaps.append(remote(hbuf.at[h // 2, c], hbuf.at[h // 2, c], h_send.at[r - 1],
                            h_recv.at[r - 1], (s, peer)))
    for copy in swaps:
        copy.wait_recv()
    result = hbuf[0].reshape(gk_ref.shape).astype(F32)
    for r in range(1, m // 2):
        result = result + hbuf[r].reshape(gk_ref.shape).astype(F32)
    gk_ref[...] = result
    for copy in pending:
        copy.wait_send()


def write_out(gq_in, gw_in, gk_in, gq_ref, gw_ref, gk_ref):
    gq_ref[...] = gq_in[...]
    gw_ref[...] = gw_in[...]
    gk_ref[...] = gk_in[...]


def solution(mesh):
    n, m = mesh.shape["seq"], mesh.shape["head"]

    def on_device(q_latent, kv_latent, normalizer, q_index, k_index, index_weight, span_pos):
        rows, heads, latent = q_latent.shape
        iheads, idim = q_index.shape[1:]
        half = rows // 2
        span = rows * n // span_pos.shape[0]
        pieces = 3 if latent % 96 == 0 else 1
        peers = max(m // 2 - 1, 1)
        V = pltpu.VMEM
        D = pltpu.SemaphoreType.DMA
        scratch = [
            V((n, 2, latent // 2, rows), BF16), V((n, 2, half, idim), BF16),
            V((heads, latent, rows), BF16), V((rows * heads, latent), BF16),
            V((rows * heads, rows), F32), V((rows * iheads, rows), F32),
            V((rows * heads, 2 * rows), F32), V((rows * iheads, rows), F32),
            V((n, rows * iheads, rows), F32),
            V((n, 2, half, rows), F32), V((n, 2, half, rows), BF16),
            V((n, half, rows), F32), V((n, half, rows), BF16),
            V((n, half, rows), F32), V((n, half, rows), BF16),
            V((n, peers, half, rows), F32), V((n, peers, half, rows), BF16),
            V((n, half, rows), F32), V((n, half, rows), F32),
            V((2, n, half, rows), BF16), V((rows * iheads, n * rows), BF16),
            V((rows * iheads, rows), F32),
            V((n, 2, half, idim), BF16), V((n, half, idim), BF16), V((n - 1, half, idim), BF16),
            V((n - 1, half, idim), BF16), V((m // 2, 2, half, idim), BF16),
            D((heads,)), D((n, pieces + 1)), D((n, pieces + 1)), D((n, pieces + 1)),
            D((n, pieces + 1)), D((n, 2)), D((n, 2)),
            D((n, peers, 2)), D((n, peers, 2)), D((1,)), D((1,)), D((n,)), D((n,)),
            D((n - 1,)), D((n - 1,)), D((m - 1,)), D((m - 1,)),
        ]
        vmem = pl.BlockSpec(memory_space=pltpu.VMEM)
        results = pl.pallas_call(
            functools.partial(kernel, n, m, heads, iheads, span, pieces),
            out_shape=(
                jax.ShapeDtypeStruct((rows * iheads, idim), F32),
                jax.ShapeDtypeStruct((iheads, rows), F32),
                jax.ShapeDtypeStruct((rows, idim), F32),
            ),
            in_specs=[pl.BlockSpec(memory_space=pl.ANY)] + [vmem] * 5 + [pl.BlockSpec(memory_space=pltpu.SMEM)],
            out_specs=(vmem, vmem, vmem),
            scratch_shapes=scratch,
            compiler_params=pltpu.CompilerParams(
                collective_id=0, has_side_effects=True, vmem_limit_bytes=60 * 2 ** 20
            ),
        )(
            q_latent.transpose(1, 2, 0), kv_latent.T.reshape(2, latent // 2, rows),
            normalizer.T, q_index.reshape(rows * iheads, idim),
            k_index.reshape(2, half, idim), index_weight.T, span_pos,
        )
        gq, gw, gk = pl.pallas_call(
            write_out,
            out_shape=tuple(jax.ShapeDtypeStruct(x.shape, x.dtype) for x in results),
            in_specs=[vmem] * 3,
            out_specs=(vmem,) * 3,
        )(*results)
        return gq.reshape(rows, iheads, idim), gw.T, gk

    in_specs = (
        P("seq", "head", None), P("seq", None), P("seq", "head"), P("seq", "head", None),
        P("seq", None), P("seq", "head"), P(),
    )
    out_specs = (P("seq", "head", None), P("seq", "head"), P("seq", None))
    return jax.shard_map(
        on_device, mesh=mesh, in_specs=in_specs, out_specs=out_specs, check_vma=False
    )
```
